768 devices in a mesh: seq: 8 (over y), exp: 48 (over z, x), enc: 2 (over core).
Axes of the slice: x: 4, y: 8, z: 12, core: 2. Of those that a mesh axis runs over, the one named last changes fastest.
Arguments:
- patches: bfloat16 [48, 16, 68, 1152], P('exp', ('seq', 'enc')), may hold values from -6 to 6
- image_counts: int32 [48, 16], P('exp'), may hold values from 1 to 17, 256 in all within a row
- image_order: int32 [48, 16], P('exp'), may hold values from 0 to 15, each once within a row
- w_merge: bfloat16 [4608, 3456], P(None, ('seq', 'enc')), may hold values from -0.09375 to 0.09375
- w_proj_out: bfloat16 [8, 2, 216, 7168], P(None, 'enc', None, 'seq'), may hold values from -0.109375 to 0.109375
- routes: int32 [12288, 8], P(('exp', 'enc')), may hold values from 0 to 383, all different within a row; in each aligned block of 128 rows (0 to 127, 128 to 255, ...) at most 3 rows name the same one
- route_weight: float32 [12288, 8], P(('exp', 'enc')), may hold values from 0.2 to 1
- expert_place: int32 [384], replicated, may hold values from -1 to 47, as said below
- w_gate: bfloat16 [48, 7168, 1024], P('exp', None, 'seq'), may hold values from -0.0625 to 0.0625
- w_up: bfloat16 [48, 7168, 1024], P('exp', None, 'seq'), may hold values from -0.0625 to 0.0625
- w_down: bfloat16 [48, 1024, 7168], P('exp', 'seq'), may hold values from -0.1875 to 0.1875
Outputs:
- hidden_out: bfloat16 [12288, 7168], P(('exp', 'enc'), 'seq')
- expert_load: float32 [48, 2], P('exp', 'enc')
The draws below stay inside these ranges and needn't reach their ends.
Inputs may be any that keep to these rules, and one draw needn't show every extreme that they name: `image_counts`: in each row the counts sum to 256 and the largest is exactly 17. `image_order`: each row is a permutation of 0 to 15. `routes`: each row names 8 different experts; among the 128 rows of one device no expert is named by more than 3 rows, a bound that some block reaches. `expert_place`: each of 0 to 47 appears exactly once; every other entry is -1.
All inputs are finite; a program needn't handle non-finite values.
Results may differ from the reference program's by a relative error of at most 0.014.
Values may be sent and summed in bfloat16 or wider, within the bound.
No kernel may reach another device: no remote copies, remote signals or barrier semaphores. Data moves between devices by JAX's collectives and lax.ppermute only.
A program may use at most 128 MiB of HBM per device.

```python
import math
from functools import partial
import jax
import jax.numpy as jnp
import numpy as np
from jax import lax

D = 7168
VIT = 1152
ALL_EXPERTS = 384
TOP = 8
MERGE = 4
PROJ_H = 3456
EXP_H = 1024
CAP = 3
TOK_DEV = 128
SHARDS = 16
SEQ_TOK = 256
IMG_CAP = 17
TOKENS = 12288
EXPERTS = 48
N_SEQ = 8
N_EXP = 48
N_ENC = 2


def draw_expert_place(key, part):
    shuffled = jax.random.permutation(jax.random.fold_in(key, 7), ALL_EXPERTS)
    numbers = jnp.arange(ALL_EXPERTS, dtype=jnp.int32)
    holder = jnp.where(numbers < EXPERTS, numbers, -1).astype(jnp.int32)
    return jnp.zeros((ALL_EXPERTS,), jnp.int32).at[shuffled].set(holder)


def levels(own_key, shape, cuts, low, largest):
    factor_of, own = 1.0, jax.random.fold_in(own_key, 6)
    for dim, parts in cuts:
        heights = jnp.exp(jax.random.uniform(jax.random.fold_in(own, dim), (parts,), jnp.float32, low / len(cuts), largest / len(cuts)))
        factor_of = factor_of * jnp.repeat(heights, shape[dim] // parts).reshape([-1 if axis == dim else 1 for axis in range(len(shape))])
    return factor_of


def length_profile(amount, total, reach, slope):
    loads = [(1 << 20) // math.isqrt(rank ** slope) + 1 for rank in range(2, amount + 1)]
    spare, given = total - reach - (amount - 1), [1] * (amount - 1)
    while spare > 0:
        free = [i for i in range(amount - 1) if given[i] < reach]
        whole, remaining = sum([loads[i] for i in free]), spare
        for i in free:
            addition = min(reach - given[i], max(1, remaining * loads[i] // whole), spare)
            given[i] = given[i] + addition
            spare = spare - addition
    return np.array([reach] + given)


def ragged(rng, count, total, limit, skew):
    if count == 2:
        one = jax.random.randint(rng, (), max(1, total - limit), min(limit, total - 1) + 1)
        return jnp.stack([one, total - one])
    tallies = jnp.asarray(length_profile(count, total, limit, skew), jnp.int32)
    twos = (count - 1) // 2
    donor, sink = tallies[1:1 + 2 * twos:2], tallies[2:2 + 2 * twos:2]
    room = jnp.minimum(donor - 1, limit - sink)
    shifted = jax.random.randint(jax.random.fold_in(rng, 1), (twos,), 0, 1 << 20) % (room + 1)
    tallies = tallies.at[1:1 + 2 * twos:2].set(donor - shifted).at[2:2 + 2 * twos:2].set(sink + shifted)
    return tallies[jax.random.permutation(jax.random.fold_in(rng, 2), count)]


def routed_block(rng, own, number, rows, amount, top, bound, slope):
    order = jax.random.permutation(rng, amount)
    heavy_load, ordinary = portions_of(amount, rows * top, bound, slope, True), portions_of(amount, rows * top, bound, slope, False)
    places = jnp.arange(amount)

    def named(tallies, rotation):
        used = int((tallies > 0).sum())
        fixed = max(1, used // 4)
        moved = fixed + (places - fixed + rotation * (used - fixed)) % max(1, amount - fixed)
        return jnp.zeros((amount,), jnp.int32).at[order[jnp.where(places < fixed, places, moved)]].set(jnp.asarray(tallies, jnp.int32))

    tallies = jnp.where(number % 4 == 0, named(heavy_load, number // 4), named(ordinary, number - number // 4 - 1))
    mixed = jax.random.permutation(jax.random.fold_in(own, 3), amount)
    donor, taker = mixed[0:amount // 2 * 2:2], mixed[1:amount // 2 * 2:2]
    room = jnp.minimum(tallies[donor] - 1, bound - tallies[taker]) // 2
    room = jnp.where((donor == order[0]) | (taker == order[0]) | (tallies[taker] == 0), 0, jnp.maximum(room, 0))
    moved = jax.random.randint(jax.random.fold_in(own, 4), (amount // 2,), 0, 1 << 20) % (room + 1)
    tallies = tallies.at[donor].add(-moved).at[taker].add(moved)
    members = jnp.searchsorted(jnp.cumsum(tallies), jnp.arange(rows * top), side="right").astype(jnp.int32)
    table = members.reshape(top, rows).T
    table = table[jax.random.permutation(jax.random.fold_in(own, 1), rows)]
    rotation = jax.random.randint(jax.random.fold_in(own, 2), (rows, 1), 0, top)
    return jnp.take_along_axis(table, (jnp.arange(top)[None, :] + rotation) % top, axis=1)


def portions_of(amount, total, most, slope, full):
    loads = [(1 << 20) // math.isqrt(rank ** slope) + 1 for rank in range(1, amount + 1)]
    largest = most if full else min(most, max(-(-total // amount), total * loads[0] // sum(loads)))
    least = 1 if total - largest >= amount - 1 else 0
    given, surplus = [largest] + [least] * (amount - 1), total - largest - least * (amount - 1)
    while surplus > 0:
        movable = [i for i in range(1, amount) if given[i] < largest] or [i for i in range(1, amount) if given[i] < most]
        pool, budget = sum([loads[i] for i in movable]), surplus
        for i in movable:
            addition = min(most - given[i], max(1, budget * loads[i] // pool), surplus)
            given[i] = given[i] + addition
            surplus = surplus - addition
    return np.array(given)


def bell_draw(key, extent, spread, reach, pieces=(), kind=jnp.bfloat16):
    drawn = jax.random.normal(key, extent, jnp.float32) * spread
    if len(pieces) > 0:
        drawn = levels(key, extent, pieces, -0.22, 0.18) * drawn
    return jnp.clip(drawn, min=-reach, max=reach).astype(kind)


def setup_inputs(seed: int = 0) -> dict:
    streams_of = jax.random.split(jax.random.key(seed), 12)
    patches = bell_draw(streams_of[0], (N_EXP, SHARDS, MERGE * IMG_CAP, VIT), 1.0, 6.0, ((0, 48), (1, 16)))
    image_counts = jax.vmap(lambda own: ragged(own, SHARDS, SEQ_TOK, IMG_CAP, 2))(jax.random.split(streams_of[1], N_EXP)).reshape((N_EXP, SHARDS)).astype(jnp.int32)
    image_order = jax.vmap(lambda own: jax.random.permutation(own, SHARDS))(jax.random.split(streams_of[2], N_EXP)).reshape((N_EXP, SHARDS)).astype(jnp.int32)
    w_merge = bell_draw(streams_of[3], (MERGE * VIT, PROJ_H), (MERGE * VIT) ** -0.5, 0.09375, ((1, 16),))
    w_proj_out = bell_draw(streams_of[4], (N_SEQ, N_ENC, PROJ_H // (N_SEQ * N_ENC), D), PROJ_H ** -0.5, 0.109375, ((1, 2), (3, 8)))
    routes_keys = jax.random.split(jax.random.fold_in(streams_of[5], 1), TOKENS // TOK_DEV)
    routes_turns = jax.random.permutation(jax.random.fold_in(streams_of[5], 3), TOKENS // TOK_DEV)
    routes = jax.vmap(lambda own, number: routed_block(jax.random.fold_in(streams_of[5], 2), own, number, TOK_DEV, ALL_EXPERTS, TOP, CAP, 0))(routes_keys, routes_turns).reshape((TOKENS, TOP))
    route_weight = jnp.clip(0.2 + 0.8 * jax.random.uniform(streams_of[6], (TOKENS, TOP), jnp.float32) ** levels(streams_of[6], (TOKENS, TOP), ((0, 96),), -0.2, 0.2), 0.2, 1.0)
    expert_place = draw_expert_place(jax.random.fold_in(streams_of[11], 71), 0)
    w_gate = bell_draw(streams_of[8], (EXPERTS, D, EXP_H), D ** -0.5, 0.0625, ((0, 48), (2, 8)))
    w_up = bell_draw(streams_of[9], (EXPERTS, D, EXP_H), D ** -0.5, 0.0625, ((0, 48), (2, 8)))
    w_down = bell_draw(streams_of[10], (EXPERTS, EXP_H, D), EXP_H ** -0.5, 0.1875, ((0, 48), (1, 8)))
    return dict(patches=patches, image_counts=image_counts, image_order=image_order, w_merge=w_merge, w_proj_out=w_proj_out, routes=routes, route_weight=route_weight, expert_place=expert_place, w_gate=w_gate, w_up=w_up, w_down=w_down)


def layer_norm(values):
    centre_mean = lax.optimization_barrier(jnp.mean(values, axis=-1, keepdims=True))
    centred = values - centre_mean
    variance = lax.optimization_barrier(jnp.mean(centred * centred, axis=-1, keepdims=True))
    return centred * lax.rsqrt(variance + 1e-06)

def sequence_rows(counts, order, seq_len, image_cap):
    shard_total = counts.shape[0]
    shard_ids = jnp.arange(shard_total, dtype=jnp.int32)
    picked = (order[:, None] == shard_ids[None, :]).astype(jnp.int32)
    ordered = lax.optimization_barrier(jnp.sum(picked * counts[None, :], axis=1))
    run_ends = jnp.cumsum(ordered)
    run_starts = run_ends - ordered
    position = jnp.arange(seq_len, dtype=jnp.int32)
    image_slot = lax.optimization_barrier(jnp.sum((position[:, None] >= run_ends[None, :]).astype(jnp.int32), axis=1))
    selected = (image_slot[:, None] == shard_ids[None, :]).astype(jnp.int32)
    shard_id = lax.optimization_barrier(jnp.sum(selected * order[None, :], axis=1))
    first_row = lax.optimization_barrier(jnp.sum(selected * run_starts[None, :], axis=1))
    return (shard_id * image_cap + position - first_row).astype(jnp.int32)

def slot_table(routes, weights, place, n_dest, cap):
    token_count, top_count = routes.shape
    target = jnp.take(place, routes.reshape(-1), axis=0)
    onehot = (target[:, None] == jnp.arange(n_dest, dtype=jnp.int32)[None, :]).astype(jnp.int32)
    rank_here = lax.optimization_barrier(jnp.sum((jnp.cumsum(onehot, axis=0) - 1) * onehot, axis=1))
    slot_id = jnp.where(target >= 0, target * cap + rank_here, -1)
    matches = slot_id[None, :] == jnp.arange(n_dest * cap, dtype=jnp.int32)[:, None]
    token_of = jnp.arange(token_count * top_count, dtype=jnp.int32) // top_count
    slot_tok = lax.optimization_barrier(jnp.sum(jnp.where(matches, token_of[None, :], 0), axis=1)).astype(jnp.int32)
    live_slot = jnp.any(matches, axis=1)
    mixing = jnp.where(matches, weights.reshape(-1)[None, :], jnp.zeros((), weights.dtype))
    mixing = lax.optimization_barrier(jnp.sum(mixing.reshape(n_dest * cap, token_count, top_count), axis=2))
    return (slot_tok, live_slot, mixing)

def kept_bf16(values):
    return lax.optimization_barrier(values.astype(jnp.bfloat16)).astype(jnp.float32)

def reference(patches, image_counts, image_order, w_merge, w_proj_out, routes, route_weight, expert_place, w_gate, w_up, w_down):
    proj_block = PROJ_H // (N_SEQ * N_ENC)
    hidden_block = EXP_H // N_SEQ
    weight_out = w_proj_out.astype(jnp.float32)

    def project(operands):
        patch, counts, order = operands
        normed = layer_norm(patch.astype(jnp.float32)).astype(jnp.bfloat16)
        merged = normed.reshape(SHARDS * IMG_CAP, MERGE * VIT)
        inner_act = jax.nn.gelu(jnp.dot(merged, w_merge, preferred_element_type=jnp.float32), approximate=False).astype(jnp.bfloat16)
        placed = jnp.take(inner_act, sequence_rows(counts, order, SEQ_TOK, IMG_CAP), axis=0)
        blocks_in = placed.reshape(SEQ_TOK, N_SEQ, N_ENC, proj_block).astype(jnp.float32)
        partial_out = jnp.einsum('tsck,sckd->ctd', blocks_in, weight_out, precision=lax.Precision.HIGHEST)
        partial_out = kept_bf16(partial_out)
        return lax.optimization_barrier(jnp.sum(partial_out, axis=0)).astype(jnp.bfloat16)
    x_all = lax.map(project, (patches, image_counts, image_order)).reshape(TOKENS, D)
    block_count = N_EXP * N_ENC
    slot_tok, live_slot, mixing = jax.vmap(partial(slot_table, place=expert_place, n_dest=EXPERTS, cap=CAP))(routes.reshape(block_count, TOK_DEV, TOP), route_weight.reshape(block_count, TOK_DEV, TOP))
    x_blocks = x_all.reshape(block_count, TOK_DEV, D)
    slot_rows = jax.vmap(partial(jnp.take, axis=0))(x_blocks, slot_tok)
    slot_rows = jnp.where(live_slot[:, :, None], slot_rows, jnp.zeros((), jnp.bfloat16))
    slot_rows = slot_rows.reshape(block_count, EXPERTS, CAP, D).transpose(1, 0, 2, 3).reshape(EXPERTS, block_count * CAP, D)

    def expert(operands):
        inputs, gate_w, up_w, down_w = operands
        squares = lax.optimization_barrier(jnp.sum(jnp.square(inputs.astype(jnp.float32)), axis=1, keepdims=True))
        inv_rms = lax.rsqrt(squares / D + 1e-06)
        gate_sum = jnp.dot(inputs, gate_w, preferred_element_type=jnp.float32) * inv_rms
        up_sum = jnp.dot(inputs, up_w, preferred_element_type=jnp.float32) * inv_rms
        hidden = (jax.nn.silu(gate_sum) * up_sum).astype(jnp.bfloat16)
        total = jnp.zeros((inputs.shape[0], D), jnp.float32)
        for block in range(N_SEQ):
            lower = block * hidden_block
            term = jnp.dot(hidden[:, lower:lower + hidden_block], down_w[lower:lower + hidden_block], preferred_element_type=jnp.float32)
            total = total + kept_bf16(term)
        return total.astype(jnp.bfloat16)
    outputs = lax.map(expert, (slot_rows, w_gate, w_up, w_down))
    outputs = outputs.reshape(EXPERTS, block_count, CAP, D).transpose(1, 0, 2, 3).reshape(block_count, EXPERTS * CAP, D)
    combined = jnp.einsum('bst,bsd->btd', mixing, outputs.astype(jnp.float32), precision=lax.Precision.HIGHEST)
    hidden_out = (x_blocks.astype(jnp.float32) + combined).astype(jnp.bfloat16).reshape(TOKENS, D)
    filled = live_slot.astype(jnp.float32).reshape(N_EXP, N_ENC, EXPERTS, CAP)
    expert_load = lax.optimization_barrier(jnp.sum(filled, axis=(0, 3))).T * (ALL_EXPERTS / (N_EXP * TOK_DEV * TOP))
    return (hidden_out, expert_load)
```

```python
import jax
import jax.numpy as jnp
from jax import lax
from jax.sharding import PartitionSpec as P

D = 7168
ALL_EXPERTS = 384
TOP = 8
MERGE = 4
CAP = 3
MARK = 2.0**60
BF = jnp.bfloat16
F32 = jnp.float32


def layer_norm(values):
    centre_mean = jnp.mean(values, axis=-1, keepdims=True)
    centred = values - centre_mean
    variance = jnp.mean(centred * centred, axis=-1, keepdims=True)
    return centred * lax.rsqrt(variance + 1e-06)


def shift(arr, axis, step):
    n = lax.axis_size(axis)
    return lax.ppermute(arr, axis, [(i, (i + step) % n) for i in range(n)])


def swap_cores(arr):
    return lax.ppermute(arr, "enc", [(0, 1), (1, 0)])


def apart(arr):
    n = lax.axis_size("seq")
    pairs = [(i * 2, (i + 1) % n * 2) for i in range(n)]
    pairs += [(i * 2 + 1, (i - 1) % n * 2 + 1) for i in range(n)]
    return lax.ppermute(arr, ("seq", "enc"), pairs)


def dot(a, b):
    return jnp.dot(a, b, preferred_element_type=F32)


def unmix(rows, image_cap):
    full = image_cap - 1
    r = jnp.arange(rows + MERGE, dtype=jnp.int32)
    source = jnp.where(r < full * MERGE, (r % full) * MERGE + r // full, r)
    return (source[:, None] == jnp.arange(rows, dtype=jnp.int32)[None, :]).astype(BF)


def projector_rows(blocks, image_cap):
    full = image_cap - 1
    n, _, width = blocks.shape
    main = [blocks[:, m * full : (m + 1) * full].reshape(n * full, width) for m in range(MERGE)]
    last = [blocks[:, MERGE * full + m] for m in range(MERGE)]
    return jnp.concatenate([jnp.concatenate(main, 1), jnp.concatenate(last, 1)], 0)


def place_of_positions(counts, order, seq_len):
    shard_total = counts.shape[0]
    ids = jnp.arange(shard_total, dtype=jnp.int32)
    ordered = jnp.sum((order[:, None] == ids[None, :]) * counts[None, :], axis=1)
    ends = jnp.sum((ids[None, :] <= ids[:, None]) * ordered[None, :], axis=1)
    starts = ends - ordered
    p = jnp.arange(seq_len, dtype=jnp.int32)
    inside = (p[:, None] >= starts[None, :]) & (p[:, None] < ends[None, :])
    shard = jnp.sum(inside * order[None, :], axis=1)
    offset = p - jnp.sum(inside * starts[None, :], axis=1)
    return shard, offset


def slot_matrix(routes, weights, place, n_dest):
    tokens = routes.shape[0]
    slots = n_dest * CAP
    row = jnp.arange(slots, dtype=jnp.int32)
    numbers = jnp.arange(place.shape[0], dtype=jnp.int32)
    expert = jnp.sum(jnp.where(place[None, :] == (row // CAP)[:, None], numbers[None, :], 0), axis=1)
    match = routes.T[None, :, :] == expert[:, None, None]
    hit = jnp.any(match, axis=1)
    weight = jnp.sum(jnp.where(match, weights.T[None, :, :], 0.0), axis=1)
    t = jnp.arange(tokens, dtype=jnp.int32)
    before = dot(hit.astype(BF), (t[:, None] < t[None, :]).astype(BF))
    mine = hit & (before == (row % CAP).astype(F32)[:, None])
    return mine, jnp.where(mine, weight, 0.0)


def shards(
    patches,
    image_counts,
    image_order,
    w_merge,
    w_proj_out,
    routes,
    route_weight,
    expert_place,
    w_gate,
    w_up,
    w_down,
):
    n_seq = lax.axis_size("seq")
    enc_count = lax.axis_size("enc")
    exp_count = lax.axis_size("exp")
    s = lax.axis_index("seq")
    c = lax.axis_index("enc")
    image_cap = patches.shape[2] // MERGE
    tokens = routes.shape[0]
    seq_len = tokens * enc_count
    columns = w_proj_out.shape[3]
    unit_block = w_proj_out.shape[2]
    half_ring = n_seq // 2

    normed = layer_norm(patches[0, 0].astype(F32)).astype(BF)
    own = dot(unmix(normed.shape[0], image_cap), normed).astype(BF)[None]
    pair = jnp.concatenate([own, swap_cores(own)], 0)
    arrived, travelling = [pair], pair
    for k in range(1, half_ring + 1):
        if k == half_ring:
            travelling = travelling[:1]
        travelling = apart(travelling)
        arrived += [travelling, swap_cores(travelling)]
    cut = 5
    inners = []
    for group in (arrived[:cut], arrived[cut:]):
        rows = projector_rows(jnp.concatenate(group, 0), image_cap)
        inners.append(jax.nn.gelu(dot(rows, w_merge), approximate=False).astype(BF))
    inner = jnp.concatenate(inners, 0)

    shard, offset = place_of_positions(image_counts[0], image_order[0], seq_len)
    away = ((shard // enc_count - s) * (2 * c - 1)) % n_seq
    other = (shard % enc_count != c).astype(jnp.int32)
    near = jnp.where(away < half_ring, away, n_seq - away)
    spot = 2 + (near - 1) * 4 + jnp.where(away < half_ring, other, 3 - other)
    spot = jnp.where(away == 0, other, jnp.where(away == half_ring, 2 + 4 * (half_ring - 1) + other, spot))
    first = 2 + 4 * (cut // 2)
    full = image_cap - 1
    late = spot >= first
    n_group = jnp.where(late, n_seq * enc_count - first, first)
    base = jnp.where(late, first * image_cap, 0)
    inside = spot - jnp.where(late, first, 0)
    row = base + jnp.where(offset < full, inside * full + offset, n_group * full + inside)
    pick = (row[:, None] == jnp.arange(inner.shape[0], dtype=jnp.int32)[None, :]).astype(BF)
    placed = dot(pick, inner).astype(BF)

    units = lax.all_gather(placed, "seq", axis=1, tiled=True)
    partial_out = dot(units, w_proj_out.reshape(n_seq * unit_block, columns)).astype(BF)

    down_w = w_down[0]
    half_units = down_w.shape[0] // enc_count
    half = lax.dynamic_slice_in_dim(down_w, c * half_units, half_units, 0)
    half = jnp.moveaxis(half.reshape(half_units, n_seq, columns), 1, 0)
    half, partial_out = lax.optimization_barrier((half, partial_out))
    down_mine = lax.all_to_all(half, "seq", 0, 0, tiled=True)
    down_other = swap_cores(down_mine)
    down_cols = jnp.where(
        c == 0,
        jnp.concatenate([down_mine, down_other], 1),
        jnp.concatenate([down_other, down_mine], 1),
    ).reshape(-1, columns)

    halves = partial_out.reshape(enc_count, tokens, columns)
    keep = lax.dynamic_index_in_dim(halves, c, 0, keepdims=False)
    give = lax.dynamic_index_in_dim(halves, 1 - c, 0, keepdims=False)
    x_cols = (keep.astype(F32) + swap_cores(give).astype(F32)).astype(BF)

    mine, mixing = slot_matrix(routes, route_weight, expert_place, exp_count)
    slot_rows = dot(mine.astype(BF), x_cols)
    empty = ~jnp.any(mine, axis=1)
    mark_here = empty[:, None] & (jnp.arange(columns, dtype=jnp.int32) == 0)[None, :]
    slot_rows = jnp.where(mark_here, MARK, slot_rows).astype(BF)
    got = lax.all_to_all(slot_rows.reshape(exp_count, CAP, columns), "exp", 0, 0, tiled=True)
    got = got.reshape(exp_count * CAP, columns)
    live = got[:, 0].astype(F32) < MARK / 1024
    expert_load = jnp.sum(live.astype(F32)) * (ALL_EXPERTS / (exp_count * tokens * TOP))

    gate_w = w_gate[0].reshape(n_seq, columns, -1)
    up_w = w_up[0].reshape(n_seq, columns, -1)

    def terms(k, block):
        at = (s + k) % n_seq
        wide = block.astype(F32)
        return (
            dot(block, lax.dynamic_index_in_dim(gate_w, at, 0, keepdims=False)),
            dot(block, lax.dynamic_index_in_dim(up_w, at, 0, keepdims=False)),
            jnp.sum(wide * wide, axis=1, keepdims=True),
        )

    total = terms(0, got)
    right = left = got
    for k in range(1, half_ring):
        right, left = shift(right, "seq", 1), shift(left, "seq", -1)
        for step, block in ((-k, right), (k, left)):
            total = tuple(a + b for a, b in zip(total, terms(step, block)))
    cut_row = got.shape[0] // 2
    block = jnp.concatenate([shift(right[:cut_row], "seq", 1), shift(left[cut_row:], "seq", -1)], 0)
    gate_sum, up_sum, squares = (a + b for a, b in zip(total, terms(half_ring, block)))
    inv_rms = lax.rsqrt(squares / D + 1e-06)
    hidden = (jax.nn.silu(gate_sum * inv_rms) * (up_sum * inv_rms)).astype(BF)
    hidden_all = lax.all_gather(hidden, "seq", axis=1, tiled=True)
    outputs = dot(hidden_all, down_cols).astype(BF)

    returned = lax.all_to_all(outputs.reshape(exp_count, CAP, columns), "exp", 0, 0, tiled=True)
    combined = lax.dot_general(
        mixing,
        returned.reshape(exp_count * CAP, columns).astype(F32),
        (((0,), (0,)), ((), ())),
        precision=lax.Precision.HIGHEST,
    )
    hidden_out = (x_cols.astype(F32) + combined).astype(BF)
    return (hidden_out, expert_load.reshape(1, 1))


def solution(mesh):
    in_specs = (
        P("exp", ("seq", "enc"), None, None),
        P("exp", None),
        P("exp", None),
        P(None, ("seq", "enc")),
        P(None, "enc", None, "seq"),
        P(("exp", "enc"), None),
        P(("exp", "enc"), None),
        P(),
        P("exp", None, "seq"),
        P("exp", None, "seq"),
        P("exp", "seq", None),
    )
    out_specs = (P(("exp", "enc"), "seq"), P("exp", "enc"))
    return jax.shard_map(shards, mesh=mesh, in_specs=in_specs, out_specs=out_specs, check_vma=False)
```

```python
import functools

import jax
import jax.numpy as jnp
from jax import lax
from jax.experimental import pallas as pl
from jax.experimental.pallas import tpu as pltpu
from jax.sharding import PartitionSpec as P

D = 7168
ALL_EXPERTS = 384
TOP = 8
MERGE = 4
CAP = 3
MARK = 2.0**60
BF = jnp.bfloat16
F32 = jnp.float32


def layer_norm(values):
    centre_mean = jnp.mean(values, axis=-1, keepdims=True)
    centred = values - centre_mean
    variance = jnp.mean(centred * centred, axis=-1, keepdims=True)
    return centred * lax.rsqrt(variance + 1e-06)


def shift(arr, axis, step):
    n = lax.axis_size(axis)
    return lax.ppermute(arr, axis, [(i, (i + step) % n) for i in range(n)])


def swap_cores(arr):
    return lax.ppermute(arr, "enc", [(0, 1), (1, 0)])


def apart(arr, k):
    n = lax.axis_size("seq")
    pairs = [(i * 2, (i + k) % n * 2) for i in range(n)]
    pairs += [(i * 2 + 1, (i - k) % n * 2 + 1) for i in range(n)]
    return lax.ppermute(arr, ("seq", "enc"), pairs)


def dot(a, b):
    return jnp.dot(a, b, preferred_element_type=F32)


def whole(shape):
    return pl.BlockSpec(shape, lambda i, at: (0,) * len(shape))


def multiplied(x, gate_ref, up_ref):
    wide = x.astype(F32)
    lanes = gate_ref.shape[1]
    squares = sum(jnp.square(wide[:, k : k + lanes]) for k in range(0, wide.shape[1], lanes))
    return dot(x, gate_ref[...]), dot(x, up_ref[...]), squares


def absorb_kernel(n, more, at_ref, *refs):
    blocks, gates, ups = refs[:n], refs[n : 2 * n], refs[2 * n : 3 * n]
    terms = [multiplied(b[...], g, u) for b, g, u in zip(blocks, gates, ups)]
    lanes = gates[0].shape[1]
    for i in range(3):
        total = terms[0][i]
        for term in terms[1:]:
            total = total + term[i]
        if more:
            total = total + refs[3 * n][:, i * lanes : (i + 1) * lanes]
        refs[-1][:, i * lanes : (i + 1) * lanes] = total


def weight_block(rows, lanes, j):
    return pl.BlockSpec((rows, lanes), lambda i, at: (at[j], 0))


def absorb(at, blocks, w_gate, w_up, total):
    n, (rows, columns), lanes = len(blocks), blocks[0].shape, w_gate.shape[1]
    more = [] if total is None else [total]
    weights = [weight_block(columns, lanes, j) for j in range(n)]
    return pl.pallas_call(
        functools.partial(absorb_kernel, n, bool(more)),
        out_shape=jax.ShapeDtypeStruct((rows, 3 * lanes), F32),
        grid_spec=pltpu.PrefetchScalarGridSpec(
            num_scalar_prefetch=1,
            grid=(1,),
            in_specs=[whole((rows, columns))] * n + weights + weights + [whole(m.shape) for m in more],
            out_specs=whole((rows, 3 * lanes)),
        ),
        cost_estimate=pl.CostEstimate(
            flops=n * 4 * rows * columns * lanes,
            bytes_accessed=n * columns * (rows + 2 * lanes) * 2,
            transcendentals=0,
        ),
        name="absorb",
    )(at, *blocks, *[w_gate] * n, *[w_up] * n, *more)


def finish_kernel(at_ref, upper_ref, lower_ref, gate_ref, up_ref, total_ref, out_ref):
    start, lanes = 0, gate_ref.shape[1]
    for ref in (upper_ref, lower_ref):
        rows = slice(start, start + ref.shape[0])
        gate, up, squares = multiplied(ref[...], gate_ref, up_ref)
        squares = squares + total_ref[rows, 2 * lanes :]
        inv_rms = lax.rsqrt(jnp.sum(squares, axis=1, keepdims=True) / D + 1e-06)
        gate = (gate + total_ref[rows, :lanes]) * inv_rms
        up = (up + total_ref[rows, lanes : 2 * lanes]) * inv_rms
        hidden = (gate / (1.0 + jnp.exp(-gate)) * up).astype(BF)
        for k in range(out_ref.shape[0]):
            out_ref[k, rows, :] = hidden
        start += ref.shape[0]


def finish(at, upper, lower, w_gate, w_up, total, copies):
    rows, columns, lanes = total.shape[0], upper.shape[1], w_gate.shape[1]
    weight = weight_block(columns, lanes, 0)
    return pl.pallas_call(
        finish_kernel,
        out_shape=jax.ShapeDtypeStruct((copies, rows, lanes), BF),
        grid_spec=pltpu.PrefetchScalarGridSpec(
            num_scalar_prefetch=1,
            grid=(1,),
            in_specs=[whole(upper.shape), whole(lower.shape), weight, weight, whole(total.shape)],
            out_specs=whole((copies, rows, lanes)),
        ),
        cost_estimate=pl.CostEstimate(
            flops=4 * rows * columns * lanes,
            bytes_accessed=columns * (rows + 2 * lanes) * 2,
            transcendentals=rows * lanes,
        ),
        name="finish",
    )(at, upper, lower, w_gate, w_up, total)


def down_kernel(hops, at_ref, hidden_ref, own_ref, mine_ref, other_ref, out_ref, far_ref, total_ref):
    units = own_ref.shape[0]
    half = units // 2
    c = at_ref[2 * hops + 2]
    far_ref[pl.ds(pl.multiple_of(c * half, half), half), :] = mine_ref[hops * units :, :]
    far_ref[pl.ds(pl.multiple_of((1 - c) * half, half), half), :] = other_ref[hops * units :, :]
    total_ref[...] = dot(hidden_ref[at_ref[0]], own_ref[...])
    for side, ref in enumerate((mine_ref, other_ref)):
        for k in range(hops):
            block = hidden_ref[at_ref[1 + side * hops + k]]
            total_ref[...] += dot(block, ref[k * units : (k + 1) * units, :])
    total = total_ref[...] + dot(hidden_ref[at_ref[2 * hops + 1]], far_ref[...])
    out_ref[...] = total.astype(out_ref.dtype)


def down(at, hidden, w_down, mine, other, hops):
    _, rows, units = hidden.shape
    columns = mine.shape[1]
    return pl.pallas_call(
        functools.partial(down_kernel, hops),
        out_shape=jax.ShapeDtypeStruct((rows, columns), BF),
        grid_spec=pltpu.PrefetchScalarGridSpec(
            num_scalar_prefetch=1,
            grid=(1,),
            in_specs=[
                whole(hidden.shape),
                pl.BlockSpec((units, columns), lambda i, at: (0, at[0])),
                whole(mine.shape),
                whole(other.shape),
            ],
            out_specs=whole((rows, columns)),
            scratch_shapes=[pltpu.VMEM((units, columns), BF), pltpu.VMEM((rows, columns), F32)],
        ),
        cost_estimate=pl.CostEstimate(
            flops=2 * hidden.size * columns,
            bytes_accessed=2 * (hidden.size + 2 * mine.size + units * columns),
            transcendentals=0,
        ),
        name="down",
    )(at, hidden, w_down, mine, other)


def unmix(rows, image_cap):
    full = image_cap - 1
    r = jnp.arange(rows + MERGE, dtype=jnp.int32)
    source = jnp.where(r < full * MERGE, (r % full) * MERGE + r // full, r)
    return (source[:, None] == jnp.arange(rows, dtype=jnp.int32)[None, :]).astype(BF)


def projector_rows(blocks, image_cap):
    full = image_cap - 1
    n, _, width = blocks.shape
    main = [blocks[:, m * full : (m + 1) * full].reshape(n * full, width) for m in range(MERGE)]
    last = [blocks[:, MERGE * full + m] for m in range(MERGE)]
    return jnp.concatenate([jnp.concatenate(main, 1), jnp.concatenate(last, 1)], 0)


def place_of_positions(counts, order, seq_len):
    shard_total = counts.shape[0]
    ids = jnp.arange(shard_total, dtype=jnp.int32)
    ordered = jnp.sum((order[:, None] == ids[None, :]) * counts[None, :], axis=1)
    ends = jnp.sum((ids[None, :] <= ids[:, None]) * ordered[None, :], axis=1)
    starts = ends - ordered
    p = jnp.arange(seq_len, dtype=jnp.int32)
    inside = (p[:, None] >= starts[None, :]) & (p[:, None] < ends[None, :])
    shard = jnp.sum(inside * order[None, :], axis=1)
    offset = p - jnp.sum(inside * starts[None, :], axis=1)
    return shard, offset


def slot_matrix(routes, weights, place, n_dest):
    tokens = routes.shape[0]
    slots = n_dest * CAP
    row = jnp.arange(slots, dtype=jnp.int32)
    numbers = jnp.arange(place.shape[0], dtype=jnp.int32)
    expert = jnp.sum(jnp.where(place[None, :] == (row // CAP)[:, None], numbers[None, :], 0), axis=1)
    match = routes.T[None, :, :] == expert[:, None, None]
    hit = jnp.any(match, axis=1)
    weight = jnp.sum(jnp.where(match, weights.T[None, :, :], 0.0), axis=1)
    t = jnp.arange(tokens, dtype=jnp.int32)
    before = dot(hit.astype(BF), (t[:, None] < t[None, :]).astype(BF))
    mine = hit & (before == (row % CAP).astype(F32)[:, None])
    return mine, jnp.where(mine, weight, 0.0)


def layer(
    patches,
    image_counts,
    image_order,
    w_merge,
    w_proj_out,
    routes,
    route_weight,
    expert_place,
    w_gate,
    w_up,
    w_down,
):
    n_seq = lax.axis_size("seq")
    enc_count = lax.axis_size("enc")
    exp_count = lax.axis_size("exp")
    s = lax.axis_index("seq")
    c = lax.axis_index("enc")
    image_cap = patches.shape[2] // MERGE
    tokens = routes.shape[0]
    seq_len = tokens * enc_count
    columns = w_proj_out.shape[3]
    unit_block = w_proj_out.shape[2]
    half_ring = n_seq // 2

    normed = layer_norm(patches[0, 0].astype(F32)).astype(BF)
    own = dot(unmix(normed.shape[0], image_cap), normed).astype(BF)[None]
    pair = jnp.concatenate([own, swap_cores(own)], 0)
    hops = [pair]
    for _ in range(half_ring):
        hops.append(apart(hops[-1], 1))
    near = jnp.concatenate(hops[1:half_ring], 0)
    near_other = swap_cores(near)
    groups = (jnp.concatenate([pair, near], 0), near_other, hops[half_ring])
    inners = []
    for group in groups:
        rows = projector_rows(group, image_cap)
        inners.append(jax.nn.gelu(dot(rows, w_merge), approximate=False).astype(BF))
    inner = jnp.concatenate(inners, 0)

    shard, offset = place_of_positions(image_counts[0], image_order[0], seq_len)
    away = ((shard // enc_count - s) * (2 * c - 1)) % n_seq
    other = (shard % enc_count != c).astype(jnp.int32)
    base = jnp.zeros_like(shard)
    inside, size = 2 * away + other, jnp.full_like(shard, groups[0].shape[0])
    mirrored = away > half_ring
    inside = jnp.where(mirrored, 2 * (n_seq - away - 1) + 1 - other, inside)
    size = jnp.where(mirrored, groups[1].shape[0], size)
    base = jnp.where(mirrored, groups[0].shape[0] * image_cap, base)
    opposite = away == half_ring
    inside = jnp.where(opposite, other, inside)
    size = jnp.where(opposite, groups[2].shape[0], size)
    base = jnp.where(opposite, (groups[0].shape[0] + groups[1].shape[0]) * image_cap, base)
    full = image_cap - 1
    row = base + jnp.where(offset < full, inside * full + offset, size * full + inside)
    pick = (row[:, None] == jnp.arange(inner.shape[0], dtype=jnp.int32)[None, :]).astype(BF)
    placed = dot(pick, inner).astype(BF)

    down_w = w_down[0]
    unit_rows = down_w.shape[0]
    toward = 1 - 2 * c

    def columns_of(device):
        return lax.dynamic_slice_in_dim(down_w, device % n_seq * columns, columns, 1)

    def after(arr, gate):
        return lax.optimization_barrier((arr, gate))[0]

    fetched = []
    for k in range(1, half_ring + 1):
        block = columns_of(s + toward * k)
        if k == half_ring:
            block = lax.dynamic_slice_in_dim(block, c * (unit_rows // 2), unit_rows // 2, 0)
        fetched.append(apart(after(block, inners[0] if k < half_ring - 1 else placed), k))

    units = lax.all_gather(placed, "seq", axis=1, tiled=True)
    partial_out = dot(units, w_proj_out.reshape(n_seq * unit_block, columns)).astype(BF)

    mine_side = jnp.concatenate(fetched, 0)
    other_side = swap_cores(mine_side)
    halves = partial_out.reshape(enc_count, tokens, columns)
    keep = lax.dynamic_index_in_dim(halves, c, 0, keepdims=False)
    give = lax.dynamic_index_in_dim(halves, 1 - c, 0, keepdims=False)
    x_cols = (keep.astype(F32) + swap_cores(give).astype(F32)).astype(BF)

    mine, mixing = slot_matrix(routes, route_weight, expert_place, exp_count)
    slot_rows = dot(mine.astype(BF), x_cols)
    empty = ~jnp.any(mine, axis=1)
    mark_here = empty[:, None] & (jnp.arange(columns, dtype=jnp.int32) == 0)[None, :]
    slot_rows = jnp.where(mark_here, MARK, slot_rows).astype(BF)
    got = lax.all_to_all(slot_rows.reshape(exp_count, CAP, columns), "exp", 0, 0, tiled=True)
    got = got.reshape(exp_count * CAP, columns)
    live = got[:, 0].astype(F32) < MARK / 1024
    expert_load = jnp.sum(live.astype(F32)) * (ALL_EXPERTS / (exp_count * tokens * TOP))

    def sources(*offsets):
        return jnp.stack([(s + k) % n_seq for k in offsets]).astype(jnp.int32)

    total = absorb(sources(0), (got,), w_gate[0], w_up[0], None)
    right = left = got
    for k in range(1, half_ring):
        left = shift(left, "seq", -1)
        right = shift(right, "seq", 1)
        total = absorb(sources(-k, k), (right, left), w_gate[0], w_up[0], total)
    cut_row = (got.shape[0] // 2 + 15) // 16 * 16
    lower = shift(left[cut_row:], "seq", -1)
    upper = shift(right[:cut_row], "seq", 1)
    hidden = finish(sources(half_ring), upper, lower, w_gate[0], w_up[0], total, n_seq)
    hidden = lax.all_to_all(hidden, "seq", 0, 0, tiled=True)
    hops_near = range(1, half_ring)
    at = jnp.concatenate([
        sources(0, *[-toward * k for k in hops_near], *[toward * k for k in hops_near], half_ring),
        c.astype(jnp.int32)[None],
    ])
    outputs = down(at, hidden, down_w, mine_side, other_side, half_ring - 1)

    returned = lax.all_to_all(outputs.reshape(exp_count, CAP, columns), "exp", 0, 0, tiled=True)
    combined = lax.dot_general(
        mixing,
        returned.reshape(exp_count * CAP, columns).astype(F32),
        (((0,), (0,)), ((), ())),
        precision=lax.Precision.HIGHEST,
    )
    hidden_out = (x_cols.astype(F32) + combined).astype(BF)
    return (hidden_out, expert_load.reshape(1, 1))


def solution(mesh):
    in_specs = (
        P("exp", ("seq", "enc"), None, None),
        P("exp", None),
        P("exp", None),
        P(None, ("seq", "enc")),
        P(None, "enc", None, "seq"),
        P(("exp", "enc"), None),
        P(("exp", "enc"), None),
        P(),
        P("exp", None, "seq"),
        P("exp", None, "seq"),
        P("exp", "seq", None),
    )
    out_specs = (P(("exp", "enc"), "seq"), P("exp", "enc"))
    return jax.shard_map(layer, mesh=mesh, in_specs=in_specs, out_specs=out_specs, check_vma=False)
```

```python
import functools

import jax
import jax.numpy as jnp
import numpy as np
from jax import lax
from jax.experimental import pallas as pl
from jax.experimental.pallas import tpu as pltpu
from jax.sharding import PartitionSpec as P

D = 7168
ALL_EXPERTS = 384
TOP = 8
MERGE = 4
CAP = 3
MARK = 2.0**60
BF = jnp.bfloat16
F32 = jnp.float32


def layer_norm(values):
    centre_mean = jnp.mean(values, axis=-1, keepdims=True)
    centred = values - centre_mean
    variance = jnp.mean(centred * centred, axis=-1, keepdims=True)
    return centred * lax.rsqrt(variance + 1e-06)


def swap_cores(arr):
    return lax.ppermute(arr, "enc", [(0, 1), (1, 0)])


def apart(arr, k):
    n = lax.axis_size("seq")
    pairs = [(i * 2, (i + k) % n * 2) for i in range(n)]
    pairs += [(i * 2 + 1, (i - k) % n * 2 + 1) for i in range(n)]
    return lax.ppermute(arr, ("seq", "enc"), pairs)


def dot(a, b):
    return jnp.dot(a, b, preferred_element_type=F32)


def whole(shape):
    return pl.BlockSpec(shape, lambda i, at: (0,) * len(shape))


def multiplied(x, gate_ref, up_ref):
    wide = x.astype(F32)
    lanes = gate_ref.shape[1]
    squares = sum(jnp.square(wide[:, k : k + lanes]) for k in range(0, wide.shape[1], lanes))
    return dot(x, gate_ref[...]), dot(x, up_ref[...]), squares


def absorb_kernel(n, more, at_ref, *refs):
    blocks, gates, ups = refs[:n], refs[n : 2 * n], refs[2 * n : 3 * n]
    terms = [multiplied(b[...], g, u) for b, g, u in zip(blocks, gates, ups)]
    lanes = gates[0].shape[1]
    for i in range(3):
        total = terms[0][i]
        for term in terms[1:]:
            total = total + term[i]
        if more:
            total = total + refs[3 * n][:, i * lanes : (i + 1) * lanes]
        refs[-1][:, i * lanes : (i + 1) * lanes] = total


def norm_kernel(patch_ref, mix_ref, out_ref):
    normed = layer_norm(patch_ref[...].astype(F32)).astype(BF)
    out_ref[...] = dot(mix_ref[...], normed).astype(BF)


def normed_rows(patch, mix):
    return pl.pallas_call(
        norm_kernel,
        out_shape=jax.ShapeDtypeStruct((mix.shape[0], patch.shape[1]), BF),
        cost_estimate=pl.CostEstimate(
            flops=2 * mix.size * patch.shape[1], bytes_accessed=4 * patch.size, transcendentals=0
        ),
        name="norm",
    )(patch, mix)


def weight_block(rows, lanes, j):
    return pl.BlockSpec((rows, lanes), lambda i, at: (at[j], 0))


def absorb(at, first, blocks, w_gate, w_up, total):
    n, (rows, columns), lanes = len(blocks), blocks[0].shape, w_gate.shape[1]
    more = [] if total is None else [total]
    weights = [weight_block(columns, lanes, first + j) for j in range(n)]
    return pl.pallas_call(
        functools.partial(absorb_kernel, n, bool(more)),
        out_shape=jax.ShapeDtypeStruct((rows, 3 * lanes), F32),
        grid_spec=pltpu.PrefetchScalarGridSpec(
            num_scalar_prefetch=1,
            grid=(1,),
            in_specs=[whole((rows, columns))] * n + weights + weights + [whole(m.shape) for m in more],
            out_specs=whole((rows, 3 * lanes)),
        ),
        cost_estimate=pl.CostEstimate(
            flops=n * 4 * rows * columns * lanes,
            bytes_accessed=n * columns * (rows + 2 * lanes) * 2,
            transcendentals=0,
        ),
        name="absorb",
    )(at, *blocks, *[w_gate] * n, *[w_up] * n, *more)


def finish_kernel(at_ref, upper_ref, lower_ref, gate_ref, up_ref, total_ref, out_ref):
    start, lanes = 0, gate_ref.shape[1]
    for ref in (upper_ref, lower_ref):
        rows = slice(start, start + ref.shape[0])
        gate, up, squares = multiplied(ref[...], gate_ref, up_ref)
        squares = squares + total_ref[rows, 2 * lanes :]
        inv_rms = lax.rsqrt(jnp.sum(squares, axis=1, keepdims=True) / D + 1e-06)
        gate = (gate + total_ref[rows, :lanes]) * inv_rms
        up = (up + total_ref[rows, lanes : 2 * lanes]) * inv_rms
        hidden = (gate / (1.0 + jnp.exp(-gate)) * up).astype(BF)
        for k in range(out_ref.shape[0]):
            out_ref[k, rows, :] = hidden
        start += ref.shape[0]


def finish(at, upper, lower, w_gate, w_up, total, copies):
    rows, columns, lanes = total.shape[0], upper.shape[1], w_gate.shape[1]
    weight = weight_block(columns, lanes, copies - 1)
    return pl.pallas_call(
        finish_kernel,
        out_shape=jax.ShapeDtypeStruct((copies, rows, lanes), BF),
        grid_spec=pltpu.PrefetchScalarGridSpec(
            num_scalar_prefetch=1,
            grid=(1,),
            in_specs=[whole(upper.shape), whole(lower.shape), weight, weight, whole(total.shape)],
            out_specs=whole((copies, rows, lanes)),
        ),
        cost_estimate=pl.CostEstimate(
            flops=4 * rows * columns * lanes,
            bytes_accessed=columns * (rows + 2 * lanes) * 2,
            transcendentals=rows * lanes,
        ),
        name="finish",
    )(at, upper, lower, w_gate, w_up, total)


def slots_kernel(keep_ref, give_ref, mine_ref, x_ref, out_ref):
    x = (keep_ref[...].astype(F32) + give_ref[...].astype(F32)).astype(BF)
    x_ref[...] = x
    mine = mine_ref[...]
    rows = dot(mine.astype(BF), x)
    empty = jnp.sum(mine, axis=1, keepdims=True) == 0
    mark_here = empty & (lax.broadcasted_iota(jnp.int32, rows.shape, 1) == 0)
    out_ref[...] = jnp.where(mark_here, MARK, rows).astype(BF)


def slots(keep, give, mine):
    return pl.pallas_call(
        slots_kernel,
        out_shape=(
            jax.ShapeDtypeStruct(keep.shape, BF),
            jax.ShapeDtypeStruct((mine.shape[0], keep.shape[1]), BF),
        ),
        cost_estimate=pl.CostEstimate(
            flops=2 * mine.size * keep.shape[1], bytes_accessed=10 * keep.size, transcendentals=0
        ),
        name="slots",
    )(keep, give, mine)


def down_kernel(pieces, at_ref, hidden_ref, own_ref, *refs):
    mine, other = refs[:pieces], refs[pieces : 2 * pieces]
    out_ref, far_ref, total_ref = refs[2 * pieces :]
    units = own_ref.shape[0]
    half = units // 2
    total_ref[...] = dot(hidden_ref[at_ref[0]], own_ref[...])
    j = 1
    for side in (mine, other):
        for ref in side[:-1]:
            for start in range(0, ref.shape[0], units):
                total_ref[...] += dot(hidden_ref[at_ref[j]], ref[start : start + units, :])
                j += 1
    c = at_ref[j + 1]
    far_ref[pl.ds(pl.multiple_of(c * half, half), half), :] = mine[-1][...]
    far_ref[pl.ds(pl.multiple_of((1 - c) * half, half), half), :] = other[-1][...]
    total = total_ref[...] + dot(hidden_ref[at_ref[j]], far_ref[...])
    out_ref[...] = total.astype(out_ref.dtype)


def down(at, hidden, w_down, mine, other):
    _, rows, units = hidden.shape
    columns = mine[0].shape[1]
    return pl.pallas_call(
        functools.partial(down_kernel, len(mine)),
        out_shape=jax.ShapeDtypeStruct((rows, columns), BF),
        grid_spec=pltpu.PrefetchScalarGridSpec(
            num_scalar_prefetch=1,
            grid=(1,),
            in_specs=[whole(hidden.shape), pl.BlockSpec((units, columns), lambda i, at: (0, at[0]))]
            + [whole(piece.shape) for piece in (*mine, *other)],
            out_specs=whole((rows, columns)),
            scratch_shapes=[pltpu.VMEM((units, columns), BF), pltpu.VMEM((rows, columns), F32)],
        ),
        cost_estimate=pl.CostEstimate(
            flops=2 * hidden.size * columns,
            bytes_accessed=2 * hidden.size + 2 * units * hidden.shape[0] * columns,
            transcendentals=0,
        ),
        name="down",
    )(at, hidden, w_down, *mine, *other)


def unmix(rows, image_cap):
    full = image_cap - 1
    r = np.arange(rows + MERGE)
    source = np.where(r < full * MERGE, (r % full) * MERGE + r // full, r)
    return jnp.asarray(source[:, None] == np.arange(rows)[None, :], BF)


def projector_rows(blocks, image_cap):
    full = image_cap - 1
    n, _, width = blocks.shape
    main = [blocks[:, m * full : (m + 1) * full].reshape(n * full, width) for m in range(MERGE)]
    last = [blocks[:, MERGE * full + m] for m in range(MERGE)]
    return jnp.concatenate([jnp.concatenate(main, 1), jnp.concatenate(last, 1)], 0)


def place_of_positions(counts, order, seq_len):
    shard_total = counts.shape[0]
    ids = jnp.arange(shard_total, dtype=jnp.int32)
    ordered = jnp.sum((order[:, None] == ids[None, :]) * counts[None, :], axis=1)
    ends = jnp.sum((ids[None, :] <= ids[:, None]) * ordered[None, :], axis=1)
    starts = ends - ordered
    p = jnp.arange(seq_len, dtype=jnp.int32)
    inside = (p[:, None] >= starts[None, :]) & (p[:, None] < ends[None, :])
    shard = jnp.sum(inside * order[None, :], axis=1)
    offset = p - jnp.sum(inside * starts[None, :], axis=1)
    return shard, offset


def slot_matrix(routes, weights, place, n_dest):
    tokens = routes.shape[0]
    slots = n_dest * CAP
    row = jnp.arange(slots, dtype=jnp.int32)
    numbers = jnp.arange(place.shape[0], dtype=jnp.int32)
    expert = jnp.sum(jnp.where(place[None, :] == (row // CAP)[:, None], numbers[None, :], 0), axis=1)
    match = routes.T[None, :, :] == expert[:, None, None]
    hit = jnp.any(match, axis=1)
    weight = jnp.sum(jnp.where(match, weights.T[None, :, :], 0.0), axis=1)
    t = jnp.arange(tokens, dtype=jnp.int32)
    before = dot(hit.astype(BF), (t[:, None] < t[None, :]).astype(BF))
    mine = hit & (before == (row % CAP).astype(F32)[:, None])
    return mine, jnp.where(mine, weight, 0.0)


def layer(
    patches,
    image_counts,
    image_order,
    w_merge,
    w_proj_out,
    routes,
    route_weight,
    expert_place,
    w_gate,
    w_up,
    w_down,
):
    n_seq = lax.axis_size("seq")
    enc_count = lax.axis_size("enc")
    exp_count = lax.axis_size("exp")
    s = lax.axis_index("seq")
    c = lax.axis_index("enc")
    image_cap = patches.shape[2] // MERGE
    tokens = routes.shape[0]
    seq_len = tokens * enc_count
    columns = w_proj_out.shape[3]
    unit_block = w_proj_out.shape[2]
    half_ring = n_seq // 2

    toward = 1 - 2 * c
    near_by = np.arange(1, half_ring)
    both_ways = toward * np.concatenate([[0], np.stack([-near_by, near_by], 1).reshape(-1), [half_ring]])
    ring_at = lax.rem(s + n_seq + both_ways, n_seq).astype(jnp.int32)
    behind = -toward * near_by
    at = lax.rem(s + n_seq + jnp.concatenate([jnp.zeros(1, jnp.int32), behind, -behind, jnp.full(1, half_ring)]), n_seq)
    at = jnp.concatenate([at, c[None]]).astype(jnp.int32)

    own = normed_rows(patches[0, 0], unmix(patches.shape[2], image_cap))[None]
    first = second = own
    near = [own]
    for _ in range(1, half_ring):
        first = apart(first, 1)
        second = apart(second, -1)
        near += [first, second]
    cut_row = (own.shape[1] // 2 + 7) // 8 * 8
    first = apart(first[:, :cut_row], 1)
    second = apart(second[:, cut_row:], -1)
    far = jnp.concatenate([first, second], 1)
    near = jnp.concatenate(near, 0)
    near_other = swap_cores(near)
    groups = (near, near_other, jnp.concatenate([far, swap_cores(far)], 0))
    inners = []
    for group in groups:
        rows = projector_rows(group, image_cap)
        inners.append(jax.nn.gelu(dot(rows, w_merge), approximate=False).astype(BF))
    inner = jnp.concatenate(inners, 0)

    shard, offset = place_of_positions(image_counts[0], image_order[0], seq_len)
    other = (shard % enc_count != c).astype(jnp.int32)
    away = ((s - shard // enc_count) * toward) % n_seq
    away = jnp.where(other == 1, (n_seq - away) % n_seq, away)
    opposite = away == half_ring
    inside = jnp.where(away < half_ring, jnp.maximum(2 * away - 1, 0), 2 * (n_seq - away))
    inside = jnp.where(opposite, other, inside)
    size = jnp.where(opposite, groups[2].shape[0], groups[0].shape[0])
    base = jnp.where(opposite, 2, other) * (groups[0].shape[0] * image_cap)
    full = image_cap - 1
    row = base + jnp.where(offset < full, inside * full + offset, size * full + inside)
    pick = (row[:, None] == jnp.arange(inner.shape[0], dtype=jnp.int32)[None, :]).astype(BF)
    placed = dot(pick, inner).astype(BF)

    down_w = w_down[0]
    unit_rows = down_w.shape[0]

    def columns_of(device):
        return lax.dynamic_slice_in_dim(down_w, device % n_seq * columns, columns, 1)

    def after(arr, gate):
        return lax.optimization_barrier((arr, gate))[0]

    fetched = []
    for k in range(1, half_ring + 1):
        block = columns_of(s + toward * k)
        if k == half_ring:
            block = lax.dynamic_slice_in_dim(block, c * (unit_rows // 2), unit_rows // 2, 0)
        fetched.append(apart(after(block, inners[0] if k < half_ring - 1 else placed), k))

    units = lax.all_gather(placed, "seq", axis=1, tiled=True)
    partial_out = dot(units, w_proj_out.reshape(n_seq * unit_block, columns)).astype(BF)

    mine_side = [jnp.concatenate(fetched[:2], 0), *fetched[2:]]
    other_side = []
    for piece in mine_side:
        other_side.append(swap_cores(piece))
    halves = partial_out.reshape(enc_count, tokens, columns)
    keep = lax.dynamic_index_in_dim(halves, c, 0, keepdims=False)
    give = lax.dynamic_index_in_dim(halves, 1 - c, 0, keepdims=False)
    give = swap_cores(give)

    mine, mixing = slot_matrix(routes, route_weight, expert_place, exp_count)
    x_cols, slot_rows = slots(keep, give, mine.astype(F32))
    got = lax.all_to_all(slot_rows.reshape(exp_count, CAP, columns), "exp", 0, 0, tiled=True)
    got = got.reshape(exp_count * CAP, columns)
    live = got[:, 0].astype(F32) < MARK / 1024
    expert_load = jnp.sum(live.astype(F32)) * (ALL_EXPERTS / (exp_count * tokens * TOP))

    total = absorb(ring_at, 0, (got,), w_gate[0], w_up[0], None)
    right = left = got
    for k in range(1, half_ring):
        left = apart(left, -1)
        right = apart(right, 1)
        total = absorb(ring_at, 2 * k - 1, (right, left), w_gate[0], w_up[0], total)
    cut_row = (got.shape[0] // 2 + 15) // 16 * 16
    lower = apart(left[cut_row:], -1)
    upper = apart(right[:cut_row], 1)
    hidden = finish(ring_at, upper, lower, w_gate[0], w_up[0], total, n_seq)
    hidden = lax.all_to_all(hidden, "seq", 0, 0, tiled=True)
    outputs = down(at, hidden, down_w, mine_side, other_side)

    returned = lax.all_to_all(outputs.reshape(exp_count, CAP, columns), "exp", 0, 0, tiled=True)
    combined = lax.dot_general(
        mixing,
        returned.reshape(exp_count * CAP, columns).astype(F32),
        (((0,), (0,)), ((), ())),
        precision=lax.Precision.HIGHEST,
    )
    hidden_out = (x_cols.astype(F32) + combined).astype(BF)
    return (hidden_out, expert_load.reshape(1, 1))


def solution(mesh):
    in_specs = (
        P("exp", ("seq", "enc"), None, None),
        P("exp", None),
        P("exp", None),
        P(None, ("seq", "enc")),
        P(None, "enc", None, "seq"),
        P(("exp", "enc"), None),
        P(("exp", "enc"), None),
        P(),
        P("exp", None, "seq"),
        P("exp", None, "seq"),
        P("exp", "seq", None),
    )
    out_specs = (P(("exp", "enc"), "seq"), P("exp", "enc"))
    return jax.shard_map(layer, mesh=mesh, in_specs=in_specs, out_specs=out_specs, check_vma=False)
```

```python
import functools

import jax
import jax.numpy as jnp
import numpy as np
from jax import lax
from jax.experimental import pallas as pl
from jax.experimental.pallas import tpu as pltpu
from jax.sharding import PartitionSpec as P

D = 7168
ALL_EXPERTS = 384
TOP = 8
MERGE = 4
CAP = 3
MARK = 2.0**60
BF = jnp.bfloat16
F32 = jnp.float32


def layer_norm(values):
    centre_mean = jnp.mean(values, axis=-1, keepdims=True)
    centred = values - centre_mean
    variance = jnp.mean(centred * centred, axis=-1, keepdims=True)
    return centred * lax.rsqrt(variance + 1e-06)


def shift(arr, axis, step):
    n = lax.axis_size(axis)
    return lax.ppermute(arr, axis, [(i, (i + step) % n) for i in range(n)])


def swap_cores(arr):
    return lax.ppermute(arr, "enc", [(0, 1), (1, 0)])


def apart(arr, k):
    n = lax.axis_size("seq")
    pairs = [(i * 2, (i + k) % n * 2) for i in range(n)]
    pairs += [(i * 2 + 1, (i - k) % n * 2 + 1) for i in range(n)]
    return lax.ppermute(arr, ("seq", "enc"), pairs)


def dot(a, b):
    return jnp.dot(a, b, preferred_element_type=F32)


def whole(shape):
    return pl.BlockSpec(shape, lambda i, at: (0,) * len(shape))


def multiplied(x, gate_ref, up_ref):
    wide = x.astype(F32)
    lanes = gate_ref.shape[1]
    squares = sum(jnp.square(wide[:, k : k + lanes]) for k in range(0, wide.shape[1], lanes))
    return dot(x, gate_ref[...]), dot(x, up_ref[...]), squares


def absorb_kernel(n, more, at_ref, *refs):
    blocks, gates, ups = refs[:n], refs[n : 2 * n], refs[2 * n : 3 * n]
    terms = [multiplied(b[...], g, u) for b, g, u in zip(blocks, gates, ups)]
    lanes = gates[0].shape[1]
    for i in range(3):
        total = terms[0][i]
        for term in terms[1:]:
            total = total + term[i]
        if more:
            total = total + refs[3 * n][:, i * lanes : (i + 1) * lanes]
        refs[-1][:, i * lanes : (i + 1) * lanes] = total


def norm_kernel(patch_ref, mix_ref, out_ref):
    normed = layer_norm(patch_ref[...].astype(F32)).astype(BF)
    out_ref[...] = dot(mix_ref[...], normed).astype(BF)


def normed_rows(patch, mix):
    return pl.pallas_call(
        norm_kernel,
        out_shape=jax.ShapeDtypeStruct((mix.shape[0], patch.shape[1]), BF),
        cost_estimate=pl.CostEstimate(
            flops=2 * mix.size * patch.shape[1], bytes_accessed=4 * patch.size, transcendentals=0
        ),
        name="norm",
    )(patch, mix)


def weight_block(rows, lanes, j):
    return pl.BlockSpec((rows, lanes), lambda i, at: (at[j], 0))


def absorb(at, first, blocks, w_gate, w_up, total):
    n, (rows, columns), lanes = len(blocks), blocks[0].shape, w_gate.shape[1]
    more = [] if total is None else [total]
    weights = [weight_block(columns, lanes, first + j) for j in range(n)]
    return pl.pallas_call(
        functools.partial(absorb_kernel, n, bool(more)),
        out_shape=jax.ShapeDtypeStruct((rows, 3 * lanes), F32),
        grid_spec=pltpu.PrefetchScalarGridSpec(
            num_scalar_prefetch=1,
            grid=(1,),
            in_specs=[whole((rows, columns))] * n + weights + weights + [whole(m.shape) for m in more],
            out_specs=whole((rows, 3 * lanes)),
        ),
        cost_estimate=pl.CostEstimate(
            flops=n * 4 * rows * columns * lanes,
            bytes_accessed=n * columns * (rows + 2 * lanes) * 2,
            transcendentals=0,
        ),
        name="absorb",
    )(at, *blocks, *[w_gate] * n, *[w_up] * n, *more)


def finish_kernel(at_ref, upper_ref, lower_ref, gate_ref, up_ref, total_ref, out_ref):
    start, lanes = 0, gate_ref.shape[1]
    for ref in (upper_ref, lower_ref):
        rows = slice(start, start + ref.shape[0])
        gate, up, squares = multiplied(ref[...], gate_ref, up_ref)
        squares = squares + total_ref[rows, 2 * lanes :]
        inv_rms = lax.rsqrt(jnp.sum(squares, axis=1, keepdims=True) / D + 1e-06)
        gate = (gate + total_ref[rows, :lanes]) * inv_rms
        up = (up + total_ref[rows, lanes : 2 * lanes]) * inv_rms
        hidden = (gate / (1.0 + jnp.exp(-gate)) * up).astype(BF)
        for k in range(out_ref.shape[0]):
            out_ref[k, rows, :] = hidden
        start += ref.shape[0]


def finish(at, upper, lower, w_gate, w_up, total, copies):
    rows, columns, lanes = total.shape[0], upper.shape[1], w_gate.shape[1]
    weight = weight_block(columns, lanes, copies - 1)
    return pl.pallas_call(
        finish_kernel,
        out_shape=jax.ShapeDtypeStruct((copies, rows, lanes), BF),
        grid_spec=pltpu.PrefetchScalarGridSpec(
            num_scalar_prefetch=1,
            grid=(1,),
            in_specs=[whole(upper.shape), whole(lower.shape), weight, weight, whole(total.shape)],
            out_specs=whole((copies, rows, lanes)),
        ),
        cost_estimate=pl.CostEstimate(
            flops=4 * rows * columns * lanes,
            bytes_accessed=columns * (rows + 2 * lanes) * 2,
            transcendentals=rows * lanes,
        ),
        name="finish",
    )(at, upper, lower, w_gate, w_up, total)


def slots_kernel(keep_ref, give_ref, mine_ref, x_ref, out_ref):
    x = (keep_ref[...].astype(F32) + give_ref[...].astype(F32)).astype(BF)
    x_ref[...] = x
    mine = mine_ref[...]
    rows = dot(mine.astype(BF), x)
    empty = jnp.sum(mine, axis=1, keepdims=True) == 0
    mark_here = empty & (lax.broadcasted_iota(jnp.int32, rows.shape, 1) == 0)
    out_ref[...] = jnp.where(mark_here, MARK, rows).astype(BF)


def slots(keep, give, mine):
    return pl.pallas_call(
        slots_kernel,
        out_shape=(
            jax.ShapeDtypeStruct(keep.shape, BF),
            jax.ShapeDtypeStruct((mine.shape[0], keep.shape[1]), BF),
        ),
        cost_estimate=pl.CostEstimate(
            flops=2 * mine.size * keep.shape[1], bytes_accessed=10 * keep.size, transcendentals=0
        ),
        name="slots",
    )(keep, give, mine)


def down_kernel(pieces, at_ref, hidden_ref, own_ref, *refs):
    mine, other = refs[:pieces], refs[pieces : 2 * pieces]
    out_ref, far_ref, total_ref = refs[2 * pieces :]
    units = own_ref.shape[0]
    half = units // 2
    total_ref[...] = dot(hidden_ref[at_ref[0]], own_ref[...])
    j = 1
    for side in (mine, other):
        for ref in side[:-1]:
            for start in range(0, ref.shape[0], units):
                total_ref[...] += dot(hidden_ref[at_ref[j]], ref[start : start + units, :])
                j += 1
    c = at_ref[j + 1]
    far_ref[pl.ds(pl.multiple_of(c * half, half), half), :] = mine[-1][...]
    far_ref[pl.ds(pl.multiple_of((1 - c) * half, half), half), :] = other[-1][...]
    total = total_ref[...] + dot(hidden_ref[at_ref[j]], far_ref[...])
    out_ref[...] = total.astype(out_ref.dtype)


def down(at, hidden, w_down, mine, other):
    _, rows, units = hidden.shape
    columns = mine[0].shape[1]
    return pl.pallas_call(
        functools.partial(down_kernel, len(mine)),
        out_shape=jax.ShapeDtypeStruct((rows, columns), BF),
        grid_spec=pltpu.PrefetchScalarGridSpec(
            num_scalar_prefetch=1,
            grid=(1,),
            in_specs=[whole(hidden.shape), pl.BlockSpec((units, columns), lambda i, at: (0, at[0]))]
            + [whole(piece.shape) for piece in (*mine, *other)],
            out_specs=whole((rows, columns)),
            scratch_shapes=[pltpu.VMEM((units, columns), BF), pltpu.VMEM((rows, columns), F32)],
        ),
        cost_estimate=pl.CostEstimate(
            flops=2 * hidden.size * columns,
            bytes_accessed=2 * hidden.size + 2 * units * hidden.shape[0] * columns,
            transcendentals=0,
        ),
        name="down",
    )(at, hidden, w_down, *mine, *other)


def unmix(rows, image_cap):
    full = image_cap - 1
    r = np.arange(rows + MERGE)
    source = np.where(r < full * MERGE, (r % full) * MERGE + r // full, r)
    return jnp.asarray(source[:, None] == np.arange(rows)[None, :], BF)


def projector_rows(blocks, image_cap):
    full = image_cap - 1
    n, _, width = blocks.shape
    main = [blocks[:, m * full : (m + 1) * full].reshape(n * full, width) for m in range(MERGE)]
    last = [blocks[:, MERGE * full + m] for m in range(MERGE)]
    return jnp.concatenate([jnp.concatenate(main, 1), jnp.concatenate(last, 1)], 0)


def place_of_positions(counts, order, seq_len):
    shard_total = counts.shape[0]
    ids = jnp.arange(shard_total, dtype=jnp.int32)
    ordered = jnp.sum((order[:, None] == ids[None, :]) * counts[None, :], axis=1)
    ends = jnp.sum((ids[None, :] <= ids[:, None]) * ordered[None, :], axis=1)
    starts = ends - ordered
    p = jnp.arange(seq_len, dtype=jnp.int32)
    inside = (p[:, None] >= starts[None, :]) & (p[:, None] < ends[None, :])
    shard = jnp.sum(inside * order[None, :], axis=1)
    offset = p - jnp.sum(inside * starts[None, :], axis=1)
    return shard, offset


def slot_matrix(routes, weights, place, n_dest):
    tokens = routes.shape[0]
    slots = n_dest * CAP
    row = jnp.arange(slots, dtype=jnp.int32)
    numbers = jnp.arange(place.shape[0], dtype=jnp.int32)
    expert = jnp.sum(jnp.where(place[None, :] == (row // CAP)[:, None], numbers[None, :], 0), axis=1)
    match = routes.T[None, :, :] == expert[:, None, None]
    hit = jnp.any(match, axis=1)
    weight = jnp.sum(jnp.where(match, weights.T[None, :, :], 0.0), axis=1)
    t = jnp.arange(tokens, dtype=jnp.int32)
    before = dot(hit.astype(BF), (t[:, None] < t[None, :]).astype(BF))
    mine = hit & (before == (row % CAP).astype(F32)[:, None])
    return mine, jnp.where(mine, weight, 0.0)


def layer(
    patches,
    image_counts,
    image_order,
    w_merge,
    w_proj_out,
    routes,
    route_weight,
    expert_place,
    w_gate,
    w_up,
    w_down,
):
    n_seq = lax.axis_size("seq")
    enc_count = lax.axis_size("enc")
    exp_count = lax.axis_size("exp")
    s = lax.axis_index("seq")
    c = lax.axis_index("enc")
    image_cap = patches.shape[2] // MERGE
    tokens = routes.shape[0]
    seq_len = tokens * enc_count
    columns = w_proj_out.shape[3]
    unit_block = w_proj_out.shape[2]
    half_ring = n_seq // 2

    near_by = np.arange(1, half_ring)
    both_ways = np.stack([-near_by, near_by], 1).reshape(-1)
    ring_at = lax.rem(s + n_seq + np.concatenate([[0], both_ways, [half_ring]]), n_seq).astype(jnp.int32)
    behind = jnp.where(c == 0, -near_by, near_by)
    at = lax.rem(s + n_seq + jnp.concatenate([jnp.zeros(1, jnp.int32), behind, -behind, jnp.full(1, half_ring)]), n_seq)
    at = jnp.concatenate([at, c[None]]).astype(jnp.int32)

    own = normed_rows(patches[0, 0], unmix(patches.shape[2], image_cap))[None]
    pair = jnp.concatenate([own, swap_cores(own)], 0)
    hops = [pair]
    for _ in range(1, half_ring + 1):
        hops.append(apart(hops[-1], 1))
    near = jnp.concatenate(hops[1:half_ring], 0)
    near_other = swap_cores(near)
    groups = (jnp.concatenate([pair, near], 0), near_other, hops[half_ring])
    inners = []
    for group in groups:
        rows = projector_rows(group, image_cap)
        inners.append(jax.nn.gelu(dot(rows, w_merge), approximate=False).astype(BF))
    inner = jnp.concatenate(inners, 0)

    shard, offset = place_of_positions(image_counts[0], image_order[0], seq_len)
    away = ((shard // enc_count - s) * (2 * c - 1)) % n_seq
    other = (shard % enc_count != c).astype(jnp.int32)
    base = jnp.zeros_like(shard)
    inside, size = 2 * away + other, jnp.full_like(shard, groups[0].shape[0])
    mirrored = away > half_ring
    inside = jnp.where(mirrored, 2 * (n_seq - away - 1) + 1 - other, inside)
    size = jnp.where(mirrored, groups[1].shape[0], size)
    base = jnp.where(mirrored, groups[0].shape[0] * image_cap, base)
    opposite = away == half_ring
    inside = jnp.where(opposite, other, inside)
    size = jnp.where(opposite, groups[2].shape[0], size)
    base = jnp.where(opposite, (groups[0].shape[0] + groups[1].shape[0]) * image_cap, base)
    full = image_cap - 1
    row = base + jnp.where(offset < full, inside * full + offset, size * full + inside)
    pick = (row[:, None] == jnp.arange(inner.shape[0], dtype=jnp.int32)[None, :]).astype(BF)
    placed = dot(pick, inner).astype(BF)

    down_w = w_down[0]
    unit_rows = down_w.shape[0]
    toward = 1 - 2 * c

    def columns_of(device):
        return lax.dynamic_slice_in_dim(down_w, device % n_seq * columns, columns, 1)

    def after(arr, gate):
        return lax.optimization_barrier((arr, gate))[0]

    fetched = []
    for k in range(1, half_ring + 1):
        block = columns_of(s + toward * k)
        if k == half_ring:
            block = lax.dynamic_slice_in_dim(block, c * (unit_rows // 2), unit_rows // 2, 0)
        fetched.append(apart(after(block, inners[0] if k < half_ring - 1 else placed), k))

    units = lax.all_gather(placed, "seq", axis=1, tiled=True)
    partial_out = dot(units, w_proj_out.reshape(n_seq * unit_block, columns)).astype(BF)

    mine_side = [jnp.concatenate(fetched[:2], 0), *fetched[2:]]
    other_side = []
    for piece in mine_side:
        other_side.append(swap_cores(piece))
    halves = partial_out.reshape(enc_count, tokens, columns)
    keep = lax.dynamic_index_in_dim(halves, c, 0, keepdims=False)
    give = lax.dynamic_index_in_dim(halves, 1 - c, 0, keepdims=False)
    give = swap_cores(give)

    mine, mixing = slot_matrix(routes, route_weight, expert_place, exp_count)
    x_cols, slot_rows = slots(keep, give, mine.astype(F32))
    got = lax.all_to_all(slot_rows.reshape(exp_count, CAP, columns), "exp", 0, 0, tiled=True)
    got = got.reshape(exp_count * CAP, columns)
    live = got[:, 0].astype(F32) < MARK / 1024
    expert_load = jnp.sum(live.astype(F32)) * (ALL_EXPERTS / (exp_count * tokens * TOP))

    total = absorb(ring_at, 0, (got,), w_gate[0], w_up[0], None)
    right = left = got
    for k in range(1, half_ring):
        left = shift(left, "seq", -1)
        right = shift(right, "seq", 1)
        total = absorb(ring_at, 2 * k - 1, (right, left), w_gate[0], w_up[0], total)
    cut_row = (got.shape[0] // 2 + 15) // 16 * 16
    lower = shift(left[cut_row:], "seq", -1)
    upper = shift(right[:cut_row], "seq", 1)
    hidden = finish(ring_at, upper, lower, w_gate[0], w_up[0], total, n_seq)
    hidden = lax.all_to_all(hidden, "seq", 0, 0, tiled=True)
    outputs = down(at, hidden, down_w, mine_side, other_side)

    returned = lax.all_to_all(outputs.reshape(exp_count, CAP, columns), "exp", 0, 0, tiled=True)
    combined = lax.dot_general(
        mixing,
        returned.reshape(exp_count * CAP, columns).astype(F32),
        (((0,), (0,)), ((), ())),
        precision=lax.Precision.HIGHEST,
    )
    hidden_out = (x_cols.astype(F32) + combined).astype(BF)
    return (hidden_out, expert_load.reshape(1, 1))


def solution(mesh):
    in_specs = (
        P("exp", ("seq", "enc"), None, None),
        P("exp", None),
        P("exp", None),
        P(None, ("seq", "enc")),
        P(None, "enc", None, "seq"),
        P(("exp", "enc"), None),
        P(("exp", "enc"), None),
        P(),
        P("exp", None, "seq"),
        P("exp", None, "seq"),
        P("exp", "seq", None),
    )
    out_specs = (P(("exp", "enc"), "seq"), P("exp", "enc"))
    return jax.shard_map(layer, mesh=mesh, in_specs=in_specs, out_specs=out_specs, check_vma=False)
```
